32 devices in a mesh: seq: 4 (over z), shard: 8 (over y, x, core).
Axes of the slice: x: 2, y: 2, z: 4, core: 2. Of those that a mesh axis runs over, the one named last changes fastest.
Arguments:
- frames: bfloat16 [8, 1024, 1536], P('shard', 'seq'), may hold values from -6 to 6
- text_states: bfloat16 [8, 64, 1536], P('shard'), may hold values from -6 to 6
- norm_gain: bfloat16 [3, 1536], P(None, 'shard'), may hold values from 0.5 to 1.5
- norm_bias: bfloat16 [3, 1536], P(None, 'shard'), may hold values from -3 to 3
- self_project: bfloat16 [3, 1536, 1536], P(None, 'shard'), may hold values from -0.15625 to 0.15625
- self_output: bfloat16 [1536, 1536], P('shard'), may hold values from -1.75 to 1.75
- cross_project: bfloat16 [3, 1536, 1536], P(None, 'shard'), may hold values from -0.15625 to 0.15625
- cross_output: bfloat16 [1536, 1536], P('shard'), may hold values from -0.625 to 0.625
- up_weight: bfloat16 [1536, 6144], P('shard'), may hold values from -0.15625 to 0.15625
- down_weight: bfloat16 [6144, 1536], P('shard'), may hold values from -0.078125 to 0.078125
- cotangent: bfloat16 [8, 1024, 1536], P('shard', 'seq'), may hold values from -6 to 6
Outputs:
- output: bfloat16 [8, 1024, 1536], P('shard', 'seq')
- frames_grad: float32 [8, 1024, 1536], P('shard', 'seq')
- text_grad: float32 [8, 64, 1536], P('shard')
- gain_grad: float32 [3, 1536], P(None, 'shard')
- bias_grad: float32 [3, 1536], P(None, 'shard')
- self_project_grad: float32 [3, 1536, 1536], P(None, 'shard')
- self_output_grad: float32 [1536, 1536], P('shard')
- cross_project_grad: float32 [3, 1536, 1536], P(None, 'shard')
- cross_output_grad: float32 [1536, 1536], P('shard')
- up_grad: float32 [1536, 6144], P('shard')
- down_grad: float32 [6144, 1536], P('shard')
The draws below stay inside these ranges and needn't reach their ends.
All inputs are finite; a program needn't handle non-finite values.
Results may differ from the reference program's by a relative error of at most 0.022.
Values may be sent and summed in bfloat16 or wider, within the bound.
No kernel may reach another device: no remote copies, remote signals or barrier semaphores. Data moves between devices by JAX's collectives and lax.ppermute only.
A program may use at most 384 MiB of HBM per device.

```python
from functools import partial
import jax
import jax.numpy as jnp
from jax import lax

D = 1536
HEADS = 24
HEAD_DIM = 64
FF = 6144
TEXT = 64
FRAMES = 1024
CLIPS = 8


def block_levels(rng, extent, shards, low, high):
    loudness, own = 1.0, jax.random.fold_in(rng, 6)
    for dim, shards_of in shards:
        draws = jnp.exp(jax.random.uniform(jax.random.fold_in(own, dim), (shards_of,), jnp.float32, low / len(shards), high / len(shards)))
        loudness = loudness * jnp.repeat(draws, extent[dim] // shards_of).reshape([-1 if axis == dim else 1 for axis in range(len(extent))])
    return loudness


def centred(rng, shape, scale, reach, pieces=(), held_as=jnp.bfloat16):
    loudness = block_levels(rng, shape, pieces, -0.22, 0.18) if pieces else 1.0
    entries = jax.random.normal(rng, shape, jnp.float32) * scale * loudness
    return jnp.minimum(jnp.maximum(entries, -reach), reach).astype(held_as)


def setup_inputs(seed: int = 0) -> dict:
    arg_keys = jax.random.split(jax.random.key(seed), 12)
    return {
        "frames": centred(arg_keys[0], (CLIPS, FRAMES, D), 1.0, 6.0, ((0, 8), (1, 4))),
        "text_states": centred(arg_keys[1], (CLIPS, TEXT, D), 1.0, 6.0, ((0, 8),)),
        "norm_gain": jnp.clip(1.0 + 0.1 * jax.random.normal(arg_keys[2], (3, D), jnp.float32), 0.5, 1.5).astype(jnp.bfloat16),
        "norm_bias": centred(arg_keys[3], (3, D), 0.5, 3.0, ((1, 8),)),
        "self_project": centred(arg_keys[4], (3, D, D), D ** -0.5, 0.15625, ((1, 8),)),
        "self_output": centred(arg_keys[5], (D, D), (D // 128) ** -0.5, 1.75, ((0, 8),)),
        "cross_project": centred(arg_keys[6], (3, D, D), D ** -0.5, 0.15625, ((1, 8),)),
        "cross_output": centred(arg_keys[7], (D, D), (D // 16) ** -0.5, 0.625, ((0, 8),)),
        "up_weight": centred(arg_keys[8], (D, FF), D ** -0.5, 0.15625, ((0, 8),)),
        "down_weight": centred(arg_keys[9], (FF, D), FF ** -0.5, 0.078125, ((0, 8),)),
        "cotangent": centred(arg_keys[10], (CLIPS, FRAMES, D), 1.0, 6.0, ((0, 8), (1, 4))),
    }


EPSILON = 1e-05
MASKED_SCORE = -1e+30
HIGHEST_PRECISION = lax.Precision.HIGHEST

@jax.custom_vjp
def low(v):
    return lax.optimization_barrier(v.astype(jnp.bfloat16)).astype(jnp.float32)

@jax.custom_vjp
def low_back(v):
    return v

def low_keep(v):
    return (low(v), None)

def low_pass(kept, grad):
    return (grad,)

def back_keep(v):
    return (v, None)

def back_low(kept, grad):
    return (low(grad),)
low.defvjp(low_keep, low_pass)
low_back.defvjp(back_keep, back_low)

def layer_norm(hidden, gain, shift):
    center = hidden - lax.optimization_barrier(jnp.mean(hidden, axis=-1, keepdims=True))
    spread = lax.rsqrt(lax.optimization_barrier(jnp.mean(center * center, axis=-1, keepdims=True)) + EPSILON)
    return center * spread * gain + shift

def product(left, right):
    return jnp.dot(left, right, precision=HIGHEST_PRECISION)

def attend_head(packed):
    queries, key_rows, value_rows = packed
    length = queries.shape[0]
    scores = jnp.einsum('qe,ke->qk', queries, key_rows, precision=HIGHEST_PRECISION) * HEAD_DIM ** (-0.5)
    scores = low_back(scores)
    row_place = lax.broadcasted_iota(jnp.int32, (length, length), 0)
    column_place = lax.broadcasted_iota(jnp.int32, (length, length), 1)
    scores = jnp.where(column_place <= row_place, scores, MASKED_SCORE)
    shares = low(jax.nn.softmax(scores, axis=-1))
    return jnp.einsum('qk,ke->qe', shares, value_rows, precision=HIGHEST_PRECISION)

def clip_layer(weights, packed):
    frames_clip, text_clip = packed
    gains, biases, self_project, self_output, cross_project, cross_output, up_weight, down_weight = weights
    scaling = HEAD_DIM ** (-0.5)
    length = frames_clip.shape[0]
    inputs_one = low(layer_norm(frames_clip, gains[0], biases[0]))
    head_split = [low(low_back(product(inputs_one, self_project[member]))).reshape(length, HEADS, HEAD_DIM).transpose(1, 0, 2) for member in range(3)]
    attended = lax.map(jax.checkpoint(attend_head), (head_split[0], head_split[1], head_split[2]))
    attended = low(low_back(attended.transpose(1, 0, 2).reshape(length, D)))
    hidden_one = frames_clip + low_back(product(attended, self_output))
    inputs_two = low(layer_norm(hidden_one, gains[1], biases[1]))
    cross_queries = low(low_back(product(inputs_two, cross_project[0]))).reshape(length, HEADS, HEAD_DIM)
    text_keys = low(low_back(product(text_clip, cross_project[1]))).reshape(TEXT, HEADS, HEAD_DIM)
    text_values = low(low_back(product(text_clip, cross_project[2]))).reshape(TEXT, HEADS, HEAD_DIM)
    scores = low_back(jnp.einsum('fhe,xhe->hfx', cross_queries, text_keys, precision=HIGHEST_PRECISION) * scaling)
    shares = low(jax.nn.softmax(scores, axis=-1))
    mixed_text = jnp.einsum('hfx,xhe->fhe', shares, text_values, precision=HIGHEST_PRECISION).reshape(length, D)
    mixed_text = low(low_back(mixed_text))
    hidden_two = hidden_one + low_back(product(mixed_text, cross_output))
    inputs_three = low(layer_norm(hidden_two, gains[2], biases[2]))
    before_act = low_back(product(inputs_three, up_weight))
    activated = low(jax.nn.gelu(before_act, approximate=False))
    return hidden_two + low_back(product(activated, down_weight))

def whole_layer(frames_all, text_all, gains, biases, self_project, self_output, cross_project, cross_output, up_weight, down_weight):
    weights = (gains, biases, self_project, self_output, cross_project, cross_output, up_weight, down_weight)
    return lax.map(jax.checkpoint(partial(clip_layer, weights)), (frames_all, text_all))

def reference(frames, text_states, norm_gain, norm_bias, self_project, self_output, cross_project, cross_output, up_weight, down_weight, cotangent):
    primals = (frames.astype(jnp.float32), text_states.astype(jnp.float32), norm_gain.astype(jnp.float32), norm_bias.astype(jnp.float32), self_project.astype(jnp.float32), self_output.astype(jnp.float32), cross_project.astype(jnp.float32), cross_output.astype(jnp.float32), up_weight.astype(jnp.float32), down_weight.astype(jnp.float32))
    result, pullback = jax.vjp(whole_layer, *primals)
    gradients = pullback(cotangent.astype(jnp.float32))
    return (result.astype(jnp.bfloat16), gradients[0], gradients[1], gradients[2], gradients[3], gradients[4], gradients[5], gradients[6], gradients[7], gradients[8], gradients[9])
```

```python
import functools

import jax
import jax.numpy as jnp
from jax import lax
from jax.experimental import pallas as pl
from jax.experimental.pallas import tpu as pltpu
from jax.sharding import PartitionSpec as P

HEAD_DIM = 64
LANES = 128
QBLOCK = 256
EPSILON = 1e-05
MASKED_SCORE = -1e30
SCALING = HEAD_DIM ** (-0.5)
BF16 = jnp.bfloat16
F32 = jnp.float32


def mm(left, right, dims=((1,), (0,))):
    return lax.dot_general(left, right, (dims, ((), ())), preferred_element_type=F32)


NT = ((1,), (1,))
TN = ((0,), (0,))


def head_masks(width):
    lane = lax.broadcasted_iota(jnp.int32, (1, width), 1) // HEAD_DIM
    return [lane == head for head in range(width // HEAD_DIM)]


def self_forward_kernel(q_ref, k_ref, v_ref, o_ref):
    length, width = q_ref.shape
    masks = head_masks(width)
    for start in range(0, length, QBLOCK):
        stop = start + QBLOCK
        query = q_ref[start:stop, :]
        keys, values = k_ref[:stop, :], v_ref[:stop, :]
        row = lax.broadcasted_iota(jnp.int32, (QBLOCK, stop), 0) + start
        visible = lax.broadcasted_iota(jnp.int32, (QBLOCK, stop), 1) <= row
        mixed = jnp.zeros((QBLOCK, width), F32)
        for mask in masks:
            own = jnp.where(mask, query, jnp.zeros_like(query))
            scores = jnp.where(visible, mm(own, keys, NT) * SCALING, MASKED_SCORE)
            weights = jnp.exp(scores - jnp.max(scores, axis=1, keepdims=True))
            shares = weights * (1.0 / jnp.sum(weights, axis=1, keepdims=True))
            mixed = jnp.where(mask, mm(shares.astype(BF16), values), mixed)
        o_ref[start:stop, :] = mixed.astype(BF16)


def self_backward_kernel(q_ref, k_ref, v_ref, g_ref, dq_ref, dk_ref, dv_ref, dk_sum, dv_sum):
    length, width = q_ref.shape
    masks = head_masks(width)
    dk_sum[...] = jnp.zeros_like(dk_sum)
    dv_sum[...] = jnp.zeros_like(dv_sum)
    for start in range(0, length, QBLOCK):
        stop = start + QBLOCK
        query, grad = q_ref[start:stop, :], g_ref[start:stop, :]
        keys, values = k_ref[:stop, :], v_ref[:stop, :]
        place = lax.broadcasted_iota(jnp.int32, (stop, QBLOCK), 1) + start
        visible = lax.broadcasted_iota(jnp.int32, (stop, QBLOCK), 0) <= place
        dq = jnp.zeros((QBLOCK, width), F32)
        for mask in masks:
            own = jnp.where(mask, query, jnp.zeros_like(query))
            own_grad = jnp.where(mask, grad, jnp.zeros_like(grad))
            scores = jnp.where(visible, mm(keys, own, NT) * SCALING, MASKED_SCORE)
            weights = jnp.exp(scores - jnp.max(scores, axis=0, keepdims=True))
            shares = weights * (1.0 / jnp.sum(weights, axis=0, keepdims=True))
            dp = mm(values, own_grad, NT)
            centre = jnp.sum(shares * dp, axis=0, keepdims=True)
            ds = (shares * (dp - centre)).astype(BF16)
            dq = jnp.where(mask, mm(ds, keys, TN), dq)
            dk_sum[:stop, :] += mm(ds, own)
            dv_sum[:stop, :] += mm(shares.astype(BF16), own_grad)
        dq_ref[start:stop, :] = (dq * SCALING).astype(BF16)
    dk_ref[...] = (dk_sum[...] * SCALING).astype(BF16)
    dv_ref[...] = dv_sum[...].astype(BF16)


def block_width(width):
    return LANES if width % LANES == 0 else width


def self_forward(queries, keys, values):
    length, width = queries.shape
    wide = block_width(width)
    spec = pl.BlockSpec((length, wide), lambda i: (0, i))
    return pl.pallas_call(
        self_forward_kernel,
        grid=(width // wide,),
        in_specs=[spec] * 3,
        out_specs=spec,
        out_shape=jax.ShapeDtypeStruct((length, width), BF16),
        name="self_forward",
    )(queries, keys, values)


def self_backward(queries, keys, values, grads):
    length, width = queries.shape
    wide = block_width(width)
    spec = pl.BlockSpec((length, wide), lambda i: (0, i))
    return pl.pallas_call(
        self_backward_kernel,
        grid=(width // wide,),
        in_specs=[spec] * 4,
        out_specs=[spec] * 3,
        out_shape=[jax.ShapeDtypeStruct((length, width), BF16)] * 3,
        scratch_shapes=[pltpu.VMEM((length, wide), F32)] * 2,
        name="self_backward",
    )(queries, keys, values, grads)


def stacked_heads(rows, masks):
    zero = jnp.zeros_like(rows)
    return jnp.concatenate([jnp.where(mask, rows, zero) for mask in masks], axis=0)


def cross_shares_of(query, keys, texts):
    scores = mm(keys, query, NT) * SCALING
    scores = scores.reshape(-1, texts, scores.shape[-1])
    weights = jnp.exp(scores - jnp.max(scores, axis=1, keepdims=True))
    return weights * (1.0 / jnp.sum(weights, axis=1, keepdims=True))


def cross_forward_kernel(q_ref, k_ref, v_ref, o_ref):
    texts, width = k_ref.shape
    masks = head_masks(width)
    keys = stacked_heads(k_ref[...], masks)
    values = stacked_heads(v_ref[...], masks)
    shares = cross_shares_of(q_ref[...], keys, texts)
    low = shares.reshape(-1, shares.shape[-1]).astype(BF16)
    o_ref[...] = mm(low, values, TN).astype(BF16)


def cross_backward_kernel(q_ref, k_ref, v_ref, g_ref, dq_ref, dk_ref, dv_ref):
    texts, width = k_ref.shape
    masks = head_masks(width)
    query, grad = q_ref[...], g_ref[...]
    keys = stacked_heads(k_ref[...], masks)
    values = stacked_heads(v_ref[...], masks)
    shares = cross_shares_of(query, keys, texts)
    dc = mm(values, grad, NT).reshape(shares.shape)
    centre = jnp.sum(shares * dc, axis=1, keepdims=True)
    ds = (shares * (dc - centre)).reshape(-1, shares.shape[-1]).astype(BF16)
    low = shares.reshape(-1, shares.shape[-1]).astype(BF16)
    dq_ref[...] = (mm(ds, keys, TN) * SCALING).astype(BF16)
    dk_full = mm(ds, query) * SCALING
    dv_full = mm(low, grad)
    dk, dv = jnp.zeros((texts, width), F32), jnp.zeros((texts, width), F32)
    for head, mask in enumerate(masks):
        rows = slice(head * texts, (head + 1) * texts)
        dk = jnp.where(mask, dk_full[rows], dk)
        dv = jnp.where(mask, dv_full[rows], dv)
    dk_ref[...] = dk.astype(BF16)
    dv_ref[...] = dv.astype(BF16)


def cross_specs(frames, texts):
    return (
        pl.BlockSpec((frames, LANES), lambda i: (0, i)),
        pl.BlockSpec((texts, LANES), lambda i: (0, i)),
    )


def cross_forward(queries, keys, values):
    frames, width = queries.shape
    frame_spec, text_spec = cross_specs(frames, keys.shape[0])
    return pl.pallas_call(
        cross_forward_kernel,
        grid=(width // LANES,),
        in_specs=[frame_spec, text_spec, text_spec],
        out_specs=frame_spec,
        out_shape=jax.ShapeDtypeStruct(queries.shape, BF16),
        name="cross_forward",
    )(queries, keys, values)


def cross_backward(queries, keys, values, grads):
    frames, width = queries.shape
    frame_spec, text_spec = cross_specs(frames, keys.shape[0])
    return pl.pallas_call(
        cross_backward_kernel,
        grid=(width // LANES,),
        in_specs=[frame_spec, text_spec, text_spec, frame_spec],
        out_specs=[frame_spec, text_spec, text_spec],
        out_shape=[jax.ShapeDtypeStruct(v.shape, BF16) for v in (queries, keys, values)],
        name="cross_backward",
    )(queries, keys, values, grads)


def norm_parts(hidden):
    centre = hidden - jnp.mean(hidden, axis=-1, keepdims=True)
    spread = lax.rsqrt(jnp.mean(centre * centre, axis=-1, keepdims=True) + EPSILON)
    return centre * spread, spread


def norm_back(unit, spread, gain, grad):
    scaled = grad * gain
    first = jnp.mean(scaled, axis=-1, keepdims=True)
    second = jnp.mean(scaled * unit, axis=-1, keepdims=True)
    return (scaled - first - unit * second) * spread


def bit_orders(count):
    bits = []
    bit = 2
    while bit < count:
        bits.append(bit)
        bit *= 2
    return bits, bits[::-1]


def order_of(bits):
    places = [0]
    for bit in reversed(bits):
        places = places + [place | bit for place in places]
    return places


def swap(values, bit, count):
    return lax.ppermute(values, "shard", [(i, i ^ bit) for i in range(count)])


def gather_partners(block, count):
    half = block.shape[0] // 2
    evens = []
    for part, bits in zip((block[:half], block[half:]), bit_orders(count)):
        held = [part]
        for bit in reversed(bits):
            held = held + [swap(piece, bit, count) for piece in held]
        evens += held
    odds = [swap(piece, 1, count) for piece in evens]
    return jnp.concatenate(odds + evens, axis=0)


def scatter_partners(odd_sums, even_sums, count):
    sums = even_sums.astype(F32) + swap(odd_sums, 1, count).astype(F32)
    half = sums.shape[0] // 2
    done = []
    for part, bits in zip((sums[:half], sums[half:]), bit_orders(count)):
        for bit in bits:
            keep = part.shape[0] // 2
            part = part[:keep] + swap(part[keep:].astype(BF16), bit, count).astype(F32)
        done.append(part)
    return jnp.concatenate(done, axis=0)


def rows_by_partner(rows, count, me):
    size = rows.shape[0] // count
    half = size // 2
    groups = []
    for odd in (1, 0):
        pieces = []
        for number, bits in enumerate(bit_orders(count)):
            for place in order_of(bits):
                start = (me ^ (place | odd)) * size + number * half
                pieces.append(lax.dynamic_slice_in_dim(rows, start, half, 0))
        groups.append(jnp.concatenate(pieces, axis=0))
    return groups


def scatter_rows(rows, count, me):
    odd_sums, even_sums = rows_by_partner(rows.astype(BF16), count, me)
    return scatter_partners(odd_sums, even_sums, count)


def ring(values, count):
    return lax.ppermute(values, "seq", [(i, (i + 1) % count) for i in range(count)])


def ring_back(values, count):
    return lax.ppermute(values, "seq", [(i, (i - 1) % count) for i in range(count)])


def gather_rows(block, count, me):
    rows = block.shape[0]
    half = rows // 2
    whole = jnp.zeros((count * rows,) + block.shape[1:], block.dtype)
    whole = lax.dynamic_update_slice_in_dim(whole, block, me * rows, 0)
    upper, lower = block[:half], block[half:]
    for step in range(1, count):
        upper, lower = ring(upper, count), ring_back(lower, count)
        source = (me - step) % count
        whole = lax.dynamic_update_slice_in_dim(whole, upper, source * rows, 0)
        source = (me + step) % count
        whole = lax.dynamic_update_slice_in_dim(whole, lower, source * rows + half, 0)
    return whole


def gather_columns(block, count, me):
    width = block.shape[-1]
    axis = block.ndim - 1
    whole = jnp.zeros(block.shape[:-1] + (count * width,), F32)
    piece = block
    for step in range(count):
        source = (me - step) % count
        whole = lax.dynamic_update_slice_in_dim(whole, piece.astype(F32), source * width, axis)
        if step < count - 1:
            piece = ring(piece, count)
    return whole


def body(
    n_seq,
    n_shard,
    frames,
    text_states,
    norm_gain,
    norm_bias,
    self_project,
    self_output,
    cross_project,
    cross_output,
    up_weight,
    down_weight,
    cotangent,
):
    seq_me = lax.axis_index("seq")
    shard_me = lax.axis_index("shard")
    own = frames[0]
    text = text_states[0]
    cot = cotangent[0]
    rows, width = own.shape
    group = width // n_seq
    shard_rows = self_project.shape[1]

    all_low = gather_rows(own, n_seq, seq_me)

    params = lax.all_gather(
        jnp.concatenate([norm_gain, norm_bias], axis=0), "shard", axis=1, tiled=True
    ).astype(F32)
    gains, biases = params[:3], params[3:]

    columns = lax.dynamic_slice_in_dim(
        jnp.concatenate([self_project, cross_project[1:]], axis=0), seq_me * group, group, 2
    )
    columns = lax.all_gather(columns, "shard", axis=1, tiled=True)
    whole_weights = lax.all_gather(
        jnp.stack([self_output, cross_project[0], cross_output]), "shard", axis=1, tiled=True
    )
    self_out_all, cross_query_all, cross_out_all = (whole_weights[j] for j in range(3))
    up_columns = lax.all_to_all(up_weight, "shard", split_axis=1, concat_axis=0, tiled=True)

    all_hidden = all_low.astype(F32)
    all_unit, _ = norm_parts(all_hidden)
    all_normed = (all_unit * gains[0] + biases[0]).astype(BF16)
    queries, keys, values = (mm(all_normed, columns[j]).astype(BF16) for j in range(3))
    mixed_heads = self_forward(queries, keys, values)
    mixed = lax.all_to_all(mixed_heads, "seq", split_axis=0, concat_axis=1, tiled=True)

    hidden = own.astype(F32)
    hidden_one = hidden + mm(mixed, self_out_all)

    text_pair = jnp.stack([mm(text, columns[j]).astype(BF16) for j in (3, 4)])
    text_pair = lax.all_gather(text_pair, "seq", axis=2, tiled=True)
    text_keys, text_values = text_pair[0], text_pair[1]
    unit_two, spread_two = norm_parts(hidden_one)
    normed_two = (unit_two * gains[1] + biases[1]).astype(BF16)
    cross_queries = mm(normed_two, cross_query_all).astype(BF16)
    cross_mixed = cross_forward(cross_queries, text_keys, text_values)
    hidden_two = hidden_one + mm(cross_mixed, cross_out_all)

    unit_three, spread_three = norm_parts(hidden_two)
    normed_three = (unit_three * gains[2] + biases[2]).astype(BF16)
    cot_all = gather_partners(cot, n_shard)
    normed_all = gather_partners(normed_three, n_shard)
    pre_act = mm(normed_all, up_columns)
    share = 0.5 * (1.0 + lax.erf(pre_act * (0.5**0.5)))
    activated = (pre_act * share).astype(BF16)
    slope = share + pre_act * jnp.exp(-0.5 * pre_act * pre_act) * ((0.5 / jnp.pi) ** 0.5)
    pre_grad = (mm(cot_all, down_weight, NT) * slope).astype(BF16)
    half = pre_grad.shape[0] // 2
    normed_three_grad = scatter_partners(
        mm(pre_grad[:half], up_columns, NT).astype(BF16),
        mm(pre_grad[half:], up_columns, NT),
        n_shard,
    )
    fed = scatter_partners(
        mm(activated[:half], down_weight).astype(BF16),
        mm(activated[half:], down_weight),
        n_shard,
    )
    output = (hidden_two + fed).astype(BF16)
    down_grad = lax.psum(mm(activated, cot_all, TN).astype(BF16), "seq")
    up_grad = mm(normed_all, pre_grad, TN).astype(BF16)
    up_grad = lax.all_to_all(up_grad, "shard", split_axis=0, concat_axis=1, tiled=True)
    up_grad = lax.psum(up_grad, "seq")
    gain_three = jnp.sum(normed_three_grad * unit_three, axis=0)
    bias_three = jnp.sum(normed_three_grad, axis=0)
    back_two = cot.astype(F32) + norm_back(unit_three, spread_three, gains[2], normed_three_grad)

    back_two_low = back_two.astype(BF16)
    cross_mixed_grad = mm(back_two_low, cross_out_all, NT).astype(BF16)
    cross_query_grad, text_key_grad, text_value_grad = cross_backward(
        cross_queries, text_keys, text_values, cross_mixed_grad
    )
    normed_two_grad = mm(cross_query_grad, cross_query_all, NT)
    gain_two = jnp.sum(normed_two_grad * unit_two, axis=0)
    bias_two = jnp.sum(normed_two_grad, axis=0)
    back_one = back_two + norm_back(unit_two, spread_two, gains[1], normed_two_grad)

    back_one_low = back_one.astype(BF16)
    mixed_grad = mm(back_one_low, self_out_all, NT).astype(BF16)
    mixed_grad = lax.all_to_all(mixed_grad, "seq", split_axis=1, concat_axis=0, tiled=True)
    head_grads = self_backward(queries, keys, values, mixed_grad)

    total = None
    gain_one = jnp.zeros((width,), F32)
    bias_one = jnp.zeros((width,), F32)
    for step in range(1, n_seq + 1):
        start = ((seq_me - step) % n_seq) * rows
        part = sum(
            mm(lax.dynamic_slice_in_dim(grad, start, rows, 0), columns[j], NT)
            for j, grad in enumerate(head_grads)
        )
        gain_one += jnp.sum(part * lax.dynamic_slice_in_dim(all_unit, start, rows, 0), axis=0)
        bias_one += jnp.sum(part, axis=0)
        total = part if total is None else part + ring(total.astype(BF16), n_seq).astype(F32)
    unit_one, spread_one = norm_parts(hidden)
    frames_grad = back_one + norm_back(unit_one, spread_one, gains[0], total)

    cross_out_grad = scatter_rows(mm(cross_mixed, back_two_low, TN), n_shard, shard_me)
    cross_query_weight = scatter_rows(mm(normed_two, cross_query_grad, TN), n_shard, shard_me)
    self_out_grad = scatter_rows(mm(mixed, back_one_low, TN), n_shard, shard_me)
    small = jnp.concatenate([cross_out_grad, cross_query_weight, self_out_grad], axis=0)
    small = lax.psum(small.astype(BF16), "seq").astype(F32)
    cross_out_grad, cross_query_weight, self_out_grad = (
        small[j * shard_rows : (j + 1) * shard_rows] for j in range(3)
    )

    text_grads = lax.psum_scatter(
        jnp.stack([text_key_grad, text_value_grad]), "seq", scatter_dimension=2, tiled=True
    )
    text_grad = lax.psum(
        mm(text_grads[0], columns[3], NT) + mm(text_grads[1], columns[4], NT), "seq"
    )
    text_weight = jnp.concatenate([mm(text, text_grads[j], TN) for j in range(2)], axis=1)
    text_weight = scatter_rows(text_weight, n_shard, shard_me)
    self_weight = jnp.concatenate([mm(all_normed, grad, TN) for grad in head_grads], axis=1)
    self_weight = scatter_rows(self_weight, n_shard, shard_me)
    pieces = jnp.stack(
        [self_weight[:, j * group : (j + 1) * group] for j in range(3)]
        + [text_weight[:, j * group : (j + 1) * group] for j in range(2)]
    ).astype(BF16)
    pieces = gather_columns(pieces, n_seq, seq_me)
    cross_weight = jnp.concatenate([cross_query_weight[None], pieces[3:]], axis=0)

    norms = jnp.stack([gain_one, gain_two, gain_three, bias_one, bias_two, bias_three])
    norms = lax.psum(norms, ("seq", "shard"))
    norms = lax.dynamic_slice_in_dim(norms, shard_me * shard_rows, shard_rows, 1)

    return (
        output[None],
        frames_grad[None],
        text_grad[None],
        norms[:3],
        norms[3:],
        pieces[:3],
        self_out_grad,
        cross_weight,
        cross_out_grad,
        up_grad.astype(F32),
        down_grad.astype(F32),
    )


def solution(mesh):
    weights = (P(None, "shard", None), P("shard", None))
    return jax.shard_map(
        functools.partial(body, mesh.shape["seq"], mesh.shape["shard"]),
        mesh=mesh,
        in_specs=(
            P("shard", "seq", None),
            P("shard", None, None),
            P(None, "shard"),
            P(None, "shard"),
            *weights,
            *weights,
            P("shard", None),
            P("shard", None),
            P("shard", "seq", None),
        ),
        out_specs=(
            P("shard", "seq", None),
            P("shard", "seq", None),
            P("shard", None, None),
            P(None, "shard"),
            P(None, "shard"),
            *weights,
            *weights,
            P("shard", None),
            P("shard", None),
        ),
        check_vma=False,
    )
```
